32 devices in a mesh: tm: 8 (over y, x, core), lat: 4 (over z).
Axes of the slice: x: 2, y: 2, z: 4, core: 2. Of those that a mesh axis runs over, the one named last changes fastest.
Arguments:
- incr_static: float32 [8, 32, 192, 128], P('tm', 'lat'), may hold values from -6 to 6
- ens_pert: bfloat16 [8, 8, 32, 192, 128], P(None, 'tm', 'lat'), may hold values from -0.59765625 to 0.59765625
- ens_weight: float32 [8, 4, 1024], P(None, 'lat', 'tm'), may hold values from -6 to 6
- column_map: int32 [32, 192], P('lat'), may hold values from 0 to 1023
- sub_steps: int32 [8], P('tm'), may hold values from 1 to 4, 24 in all
- diffusion: bfloat16 [8, 32, 192, 128], P('tm', 'lat'), may hold values from 0.0099487305 to 0.23925781
- mode_in: bfloat16 [4, 128, 128], replicated, may hold values from -0.5 to 0.5
- mode_out: bfloat16 [4, 128, 128], replicated, may hold values from -0.25 to 0.25
- model_precision: bfloat16 [8, 32, 192, 128], P('tm', 'lat'), may hold values from 0.099609375 to 1
- obs_precision: bfloat16 [8, 32, 192, 128], P('tm', 'lat'), may hold values from 0.099609375 to 1
- innovation: bfloat16 [8, 32, 192, 128], P('tm', 'lat'), may hold values from -6 to 6
Outputs:
- grad_static: float32 [8, 32, 192, 128], P('tm', 'lat')
- grad_weight: float32 [8, 4, 1024], P(None, 'lat', 'tm')
The draws below stay inside these ranges and needn't reach their ends.
Inputs may be any that keep to these rules, and one draw needn't show every extreme that they name: `column_map`: each cell names one of the 1024 weight columns of its own latitude slab. `sub_steps`: the subwindows' step counts add up to 24.
All inputs are finite; a program needn't handle non-finite values. No bound on the sum of `sub_steps` on one device may be relied on, other than what follows from the above.
Results may differ from the reference program's by a relative error of at most 0.0065.
Values may be sent and summed in bfloat16 or wider, within the bound.
A program may use at most 64 MiB of HBM per device.

```python
import math
import jax
import jax.numpy as jnp
import numpy as np
from jax import lax

LAT_DEV = 8
LON = 192
LEV = 128
MEM = 8
STEPS = 4
SUB = 8
LATS = 32
SLABS = 4
CSLAB = 1024


def place_ends(entries, rng, low, high):
    index_at = [jax.random.randint(jax.random.fold_in(rng, axis), (), 0, length) for axis, length in enumerate(entries.shape)]
    main_axis = entries.shape.index(max(entries.shape))
    neighbour = index_at[:main_axis] + [(index_at[main_axis] + 1) % entries.shape[main_axis]] + index_at[main_axis + 1:]
    return entries.at[tuple(index_at)].set(low).at[tuple(neighbour)].set(high)


def block_scale(rng, dims, pieces, low, largest):
    level, own = 1.0, jax.random.fold_in(rng, 6)
    for axis_at, shards_of in pieces:
        draws = jnp.exp(jax.random.uniform(jax.random.fold_in(own, axis_at), (shards_of,), jnp.float32, low / len(pieces), largest / len(pieces)))
        level = level * jnp.repeat(draws, dims[axis_at] // shards_of).reshape([-1 if axis == axis_at else 1 for axis in range(len(dims))])
    return level


def profile(count, total, limit, skew):
    weights = [(1 << 20) // math.isqrt(standing ** skew) + 1 for standing in range(2, count + 1)]
    surplus, holding = total - limit - (count - 1), [1] * (count - 1)
    while surplus > 0:
        free = [i for i in range(count - 1) if holding[i] < limit]
        whole, left = sum([weights[i] for i in free]), surplus
        for i in free:
            addition = min(limit - holding[i], max(1, left * weights[i] // whole), surplus)
            holding[i] = holding[i] + addition
            surplus = surplus - addition
    return np.array([limit] + holding)


def uneven_parts(rng, count, total, limit, slope):
    if count == 2:
        one = jax.random.randint(rng, (), max(1, total - limit), min(limit, total - 1) + 1)
        return jnp.stack([one, total - one])
    sizes = jnp.asarray(profile(count, total, limit, slope), jnp.int32)
    couples = (count - 1) // 2
    donor, sink = sizes[1:1 + 2 * couples:2], sizes[2:2 + 2 * couples:2]
    margin = jnp.minimum(donor - 1, limit - sink)
    passed = jax.random.randint(jax.random.fold_in(rng, 1), (couples,), 0, 1 << 20) % (margin + 1)
    sizes = sizes.at[1:1 + 2 * couples:2].set(donor - passed).at[2:2 + 2 * couples:2].set(sink + passed)
    return sizes[jax.random.permutation(jax.random.fold_in(rng, 2), count)]


def noise(stream_key, extent, scale, bound, shards=(), held_as=jnp.bfloat16):
    values = jax.random.normal(stream_key, extent, jnp.float32) * scale
    if len(shards) > 0:
        values = block_scale(stream_key, extent, shards, -0.22, 0.18) * values
    return jnp.clip(values, min=-bound, max=bound).astype(held_as)


def setup_inputs(seed: int = 0) -> dict:
    streams_of = jax.random.split(jax.random.key(seed), 12)
    incr_static = noise(streams_of[0], (SUB, LATS, LON, LEV), 1.0, 6.0, ((0, 8), (1, 4)), jnp.float32)
    ens_pert = noise(streams_of[1], (MEM, SUB, LATS, LON, LEV), 0.1, 0.59765625, ((1, 8), (2, 4)))
    ens_weight = noise(streams_of[2], (MEM, SLABS, CSLAB), 1.0, 6.0, ((1, 4), (2, 8)), jnp.float32)
    column_map = place_ends(jax.random.randint(streams_of[3], (LATS, LON), 0, CSLAB), jax.random.fold_in(streams_of[3], 1), 0, CSLAB - 1).astype(jnp.int32)
    sub_steps = uneven_parts(streams_of[4], SUB, 3 * SUB, STEPS, 0).astype(jnp.int32)
    diffusion = jnp.clip(jnp.exp(math.log(0.23925781) - 3.1800967 * jax.random.uniform(streams_of[5], (SUB, LATS, LON, LEV), jnp.float32) ** block_scale(streams_of[5], (SUB, LATS, LON, LEV), ((0, 8), (1, 4)), -0.2, 0.2)), 0.0099487305, 0.23925781).astype(jnp.bfloat16)
    mode_in = noise(streams_of[6], (STEPS, LEV, LEV), LEV ** -0.5, 0.5)
    mode_out = noise(streams_of[7], (STEPS, LEV, LEV), (4 * LEV) ** -0.5, 0.25)
    model_precision = jnp.clip(jnp.exp(math.log(1.0) - 2.306499 * jax.random.uniform(streams_of[8], (SUB, LATS, LON, LEV), jnp.float32) ** block_scale(streams_of[8], (SUB, LATS, LON, LEV), ((0, 8), (1, 4)), -0.2, 0.2)), 0.099609375, 1.0).astype(jnp.bfloat16)
    obs_precision = jnp.clip(jnp.exp(math.log(1.0) - 2.306499 * jax.random.uniform(streams_of[9], (SUB, LATS, LON, LEV), jnp.float32) ** block_scale(streams_of[9], (SUB, LATS, LON, LEV), ((0, 8), (1, 4)), -0.2, 0.2)), 0.099609375, 1.0).astype(jnp.bfloat16)
    innovation = noise(streams_of[10], (SUB, LATS, LON, LEV), 1.0, 6.0, ((0, 8), (1, 4)))
    return {"incr_static": incr_static, "ens_pert": ens_pert, "ens_weight": ens_weight, "column_map": column_map, "sub_steps": sub_steps, "diffusion": diffusion, "mode_in": mode_in, "mode_out": mode_out, "model_precision": model_precision, "obs_precision": obs_precision, "innovation": innovation}


def laplace(state_field):
    padded = jnp.pad(state_field, ((1, 1), (0, 0), (0, 0)))
    return (padded[2:] + padded[:-2] + jnp.roll(state_field, 1, axis=1)
            + jnp.roll(state_field, -1, axis=1) - 4.0 * state_field)


def vertical(smoothed, to_modes, from_modes):
    layout = smoothed.shape
    flat = smoothed.astype(jnp.bfloat16).reshape(-1, layout[-1])
    mode_values = jnp.dot(flat, to_modes, preferred_element_type=jnp.float32).astype(jnp.bfloat16)
    return jnp.dot(mode_values, from_modes, preferred_element_type=jnp.float32).reshape(layout)


def tangent(state_field, diffuse, step_count, mode_in, mode_out):
    for section in range(STEPS):
        smoothed = state_field + diffuse * laplace(state_field)
        advanced = smoothed + vertical(smoothed, mode_in[section], mode_out[section])
        state_field = jnp.where(section < step_count, advanced, state_field)
    return state_field


def adjoint(state_field, diffuse, step_count, mode_in, mode_out):
    for section in reversed(range(STEPS)):
        coupled = state_field + vertical(state_field, mode_out[section].T, mode_in[section].T)
        advanced = coupled + laplace(diffuse * coupled)
        state_field = jnp.where(section < step_count, advanced, state_field)
    return state_field


def reference(incr_static, ens_pert, ens_weight, column_map, sub_steps, diffusion, mode_in, mode_out,
              model_precision, obs_precision, innovation):
    row_slab = (jnp.arange(LATS, dtype=jnp.int32) // LAT_DEV).astype(jnp.int32)
    member_weight = jnp.take_along_axis(ens_weight[:, row_slab, :], column_map[None], axis=2)
    segment_ids = (row_slab[:, None] * CSLAB + column_map).reshape(-1)

    def start_of(window):
        pert_here = lax.dynamic_index_in_dim(ens_pert, window, 1, keepdims=False)
        return incr_static[window] + jnp.sum(pert_here.astype(jnp.float32) * member_weight[..., None], axis=0)

    def run(window):
        return tangent(start_of(window), diffusion[window].astype(jnp.float32), sub_steps[window], mode_in, mode_out)

    windows = jnp.arange(SUB, dtype=jnp.int32)
    end_state = lax.map(run, windows)

    def jump_of(window):
        earlier = lax.dynamic_index_in_dim(end_state, jnp.maximum(window - 1, 0), 0, keepdims=False)
        earlier = jnp.where(window > 0, earlier, jnp.zeros_like(earlier))
        return model_precision[window].astype(jnp.float32) * (start_of(window) - earlier)

    def gradient_of(window):
        own_jump = jump_of(window)
        next_jump = jump_of(jnp.minimum(window + 1, SUB - 1))
        next_jump = jnp.where(window + 1 < SUB, next_jump, jnp.zeros_like(next_jump))
        misfit = obs_precision[window].astype(jnp.float32) * (end_state[window] - innovation[window].astype(jnp.float32))
        gradient = own_jump + adjoint(misfit - next_jump, diffusion[window].astype(jnp.float32),
                                      sub_steps[window], mode_in, mode_out)
        pert_here = lax.dynamic_index_in_dim(ens_pert, window, 1, keepdims=False)
        contrib = jnp.sum(pert_here.astype(jnp.float32) * gradient[None], axis=-1)
        summed = jax.ops.segment_sum(contrib.reshape(MEM, -1).T, segment_ids, num_segments=SLABS * CSLAB)
        return gradient, summed.T.reshape(MEM, SLABS, CSLAB)

    gradients, partial_terms = lax.map(gradient_of, windows)
    return gradients, ens_weight + jnp.sum(partial_terms, axis=0)
```

```python
import jax
import jax.numpy as jnp
from jax import lax
from jax.experimental import pallas as pl
from jax.experimental.pallas import tpu as pltpu
from jax.sharding import PartitionSpec as P

MESH = pl.DeviceIdType.MESH
F32, BF16 = jnp.float32, jnp.bfloat16
LAST = (((1,), (1,)), ((), ()))


def halves(x):
    high = x.astype(BF16)
    low = (x - high.astype(F32)).astype(BF16)
    return jnp.concatenate([high, low], axis=0)


def kernel(
    tm_count, lat_count, sizes,
    steps_ref, incr_h, pert_h, weight_h, cmap_h, diff_h, min_h, mout_h, prec_h, obs_h, innov_h,
    grad_h, gw_ref,
    incr, pert, gathered, cmap, cpad, diff, m_in, m_out, prec, obs, innov,
    onehot, start, start_bf, a_buf, b_buf, state_halo, start_next, prec_next,
    end_bf, end_prev, u_buf, seed_bf, seed_halo, c_buf, w_buf, mw_t, contrib, grad,
    term_send, term_recv, local_sem, send_sem, recv_sem, ag_send, ag_recv, rs_send, rs_recv,
):
    H, R, LON, LEV, MEM, CW = sizes
    C = CW * tm_count
    PAD = cpad.shape[1]
    me_t, me_l = lax.axis_index("tm"), lax.axis_index("lat")
    has_up, has_down = me_l > 0, me_l < lat_count - 1
    has_prev, has_next = me_t > 0, me_t < tm_count - 1

    def local(i, src, dst):
        return pltpu.make_async_copy(src, dst, local_sem.at[i])

    def remote(i, src, dst, tm, lat):
        return pltpu.make_async_remote_copy(
            src_ref=src, dst_ref=dst, send_sem=send_sem.at[i], recv_sem=recv_sem.at[i],
            device_id=(tm, lat), device_id_type=MESH,
        )

    loads = dict(
        weight=local(0, weight_h, gathered.at[me_t]),
        cmap=local(1, cmap_h, cmap),
        pert=local(2, pert_h.at[:, 0], pert),
        incr=local(3, incr_h.at[0], incr),
        diff=local(4, diff_h.at[0], diff.at[pl.ds(H, R)]),
        m_in=local(5, min_h, m_in),
        m_out=local(6, mout_h, m_out),
        prec=local(7, prec_h.at[0], prec),
        obs=local(8, obs_h.at[0], obs),
        innov=local(9, innov_h.at[0], innov),
    )
    for copy in loads.values():
        copy.start()

    barrier = pltpu.get_barrier_semaphore()
    for d in range(1, tm_count):
        pl.semaphore_signal(barrier, inc=1, device_id=(lax.rem(me_t + d, tm_count), me_l), device_id_type=MESH)

    @pl.when(has_up)
    def _():
        pl.semaphore_signal(barrier, inc=1, device_id=(me_t, me_l - 1), device_id_type=MESH)

    @pl.when(has_down)
    def _():
        pl.semaphore_signal(barrier, inc=1, device_id=(me_t, me_l + 1), device_id_type=MESH)

    @pl.when(jnp.logical_not(has_up))
    def _():
        diff[0:H] = jnp.zeros((H, LON, LEV), BF16)
        state_halo[0] = jnp.zeros((H, LON, LEV), BF16)
        seed_halo[0] = jnp.zeros((H, LON, LEV), BF16)

    @pl.when(jnp.logical_not(has_down))
    def _():
        diff[H + R:2 * H + R] = jnp.zeros((H, LON, LEV), BF16)
        state_halo[1] = jnp.zeros((H, LON, LEV), BF16)
        seed_halo[1] = jnp.zeros((H, LON, LEV), BF16)

    @pl.when(jnp.logical_not(has_prev))
    def _():
        end_prev[...] = jnp.zeros((R, LON, LEV), BF16)

    @pl.when(jnp.logical_not(has_next))
    def _():
        start_next[...] = jnp.zeros((R, LON, LEV), BF16)
        prec_next[...] = jnp.zeros((R, LON, LEV), BF16)

    loads["weight"].wait()
    pl.semaphore_wait(barrier, tm_count - 1 + has_up.astype(jnp.int32) + has_down.astype(jnp.int32))

    def spread(d):
        peer = lax.rem(me_t + d, tm_count)
        return pltpu.make_async_remote_copy(
            src_ref=gathered.at[me_t], dst_ref=gathered.at[me_t], send_sem=ag_send.at[d],
            recv_sem=ag_recv.at[d], device_id=(peer, me_l), device_id_type=MESH,
        )

    def term(d):
        peer = lax.rem(me_t + d, tm_count)
        return pltpu.make_async_remote_copy(
            src_ref=term_send.at[peer], dst_ref=term_recv.at[me_t], send_sem=rs_send.at[d],
            recv_sem=rs_recv.at[d], device_id=(peer, me_l), device_id_type=MESH,
        )

    for d in range(1, tm_count):
        spread(d).start()

    diff_up = remote(0, diff_h.at[0, pl.ds(0, H)], diff.at[pl.ds(H + R, H)], me_t, me_l - 1)
    diff_down = remote(1, diff_h.at[0, pl.ds(R - H, H)], diff.at[pl.ds(0, H)], me_t, me_l + 1)
    prec_back = remote(2, prec_h.at[0], prec_next, me_t - 1, me_l)
    start_back = remote(3, start_bf, start_next, me_t - 1, me_l)
    state_up = remote(4, start_bf.at[pl.ds(0, H)], state_halo.at[1], me_t, me_l - 1)
    state_down = remote(5, start_bf.at[pl.ds(R - H, H)], state_halo.at[0], me_t, me_l + 1)
    end_on = remote(6, end_bf, end_prev, me_t + 1, me_l)
    seed_up = remote(7, seed_bf.at[pl.ds(0, H)], seed_halo.at[1], me_t, me_l - 1)
    seed_down = remote(8, seed_bf.at[pl.ds(R - H, H)], seed_halo.at[0], me_t, me_l + 1)

    def go(copy, there):
        @pl.when(there)
        def _():
            copy.start()

    def sent(copy, there):
        @pl.when(there)
        def _():
            copy.wait_send()

    def got(copy, there):
        @pl.when(there)
        def _():
            copy.wait_recv()

    go(diff_up, has_up)
    go(diff_down, has_down)
    go(prec_back, has_prev)

    loads["cmap"].wait()
    cpad[...] = jnp.full(cpad.shape, -1, jnp.int32)
    cpad[:, 0:LON] = cmap[...]
    contrib[...] = jnp.zeros(contrib.shape, F32)
    LANES = PAD
    CH = 128 if C % 128 == 0 else C

    def indicate(chunk, carry):
        base = pl.multiple_of(chunk * CH, CH)
        rows = lax.broadcasted_iota(jnp.int32, (CH, LANES), 0) + base
        for i in range(R):
            hit = jnp.where(rows == cpad[i:i + 1, :], 1.0, 0.0).astype(BF16)
            onehot[pl.ds(base, CH), i * LANES:(i + 1) * LANES] = hit
        return carry

    lax.fori_loop(0, C // CH, indicate, 0)

    for d in range(1, tm_count):
        spread(d).wait_recv()
    weights = jnp.concatenate([gathered[p] for p in range(tm_count)], axis=1)
    picked = jnp.dot(halves(weights), onehot[...], preferred_element_type=F32)
    mw_t[...] = jnp.transpose(picked[0:MEM] + picked[MEM:2 * MEM])

    loads["pert"].wait()
    loads["incr"].wait()

    def begin(i, carry):
        cols = mw_t[pl.ds(pl.multiple_of(i * LANES, LANES), LON), :]
        row = incr[i]
        for k in range(MEM):
            row = row + pert[k, i].astype(F32) * cols[:, k:k + 1]
        start[i] = row
        a_buf[i + H] = row
        start_bf[i] = row.astype(BF16)
        return carry

    lax.fori_loop(0, H, begin, 0)
    go(state_up, has_up)
    lax.fori_loop(H, R - H, begin, 0)
    lax.fori_loop(R - H, R, begin, 0)
    go(state_down, has_down)
    go(start_back, has_prev)

    step_count = steps_ref[0]
    loads["diff"].wait()
    loads["m_in"].wait()
    loads["m_out"].wait()

    def forward_row(n, src, dst, r):
        here = src[r]
        lap = src[r - 1] + src[r + 1] + pltpu.roll(here, 1, 0) + pltpu.roll(here, LON - 1, 0) - 4.0 * here
        smoothed = here + diff[r].astype(F32) * lap
        modes = jnp.dot(smoothed.astype(BF16), m_in[n], preferred_element_type=F32).astype(BF16)
        advanced = smoothed + jnp.dot(modes, m_out[n], preferred_element_type=F32)
        result = jnp.where(n < step_count, advanced, here)
        dst[r] = result
        return result

    def buffers(n):
        return (a_buf, b_buf) if n % 2 == 0 else (b_buf, a_buf)

    def forward_inner(n):
        src, dst = buffers(n)
        first, count = H + n + 1, R - 2 * n - 2

        def pair(i, carry):
            forward_row(n, src, dst, first + i)
            forward_row(n, src, dst, first + count // 2 + i)
            return carry

        if count > 0:
            lax.fori_loop(0, count // 2, pair, 0)

    def forward_edges(n):
        src, dst = buffers(n)

        def pair(i, carry):
            forward_row(n, src, dst, n + 1 + i)
            forward_row(n, src, dst, H + R - n - 1 + i)
            return carry

        lax.fori_loop(0, H, pair, 0)

    for n in range(H - 1):
        forward_inner(n)
    got(diff_up, has_down)
    got(diff_down, has_up)
    got(state_up, has_down)
    got(state_down, has_up)

    def widen(i, carry):
        a_buf[i] = state_halo[0, i].astype(F32)
        a_buf[i + H + R] = state_halo[1, i].astype(F32)
        return carry

    lax.fori_loop(0, H, widen, 0)
    for n in range(H - 1):
        forward_edges(n)
    loads["obs"].wait()
    loads["innov"].wait()
    got(prec_back, has_next)
    got(start_back, has_next)
    src, dst = buffers(H - 1)

    def finish_row(i):
        end = forward_row(H - 1, src, dst, i + H)
        misfit = obs[i].astype(F32) * (end - innov[i].astype(F32))
        seed = misfit - prec_next[i].astype(F32) * (start_next[i].astype(F32) - end)
        end_bf[i] = end.astype(BF16)
        u_buf[i + H] = seed
        seed_bf[i] = seed.astype(BF16)

    def finish(i, carry):
        finish_row(2 * i)
        finish_row(2 * i + 1)
        return carry

    lax.fori_loop(0, H // 2, finish, 0)
    go(seed_up, has_up)
    lax.fori_loop(H // 2, R // 2, finish, 0)
    go(seed_down, has_down)
    go(end_on, has_next)

    def couple_row(m, r):
        n = H - 1 - m
        here = u_buf[r]
        modes = lax.dot_general(here.astype(BF16), m_out[n], LAST, preferred_element_type=F32).astype(BF16)
        coupled = here + lax.dot_general(modes, m_in[n], LAST, preferred_element_type=F32)
        c_buf[m % 2, r] = coupled
        w_buf[m % 2, r] = diff[r].astype(F32) * coupled

    def spread_row(m, r):
        w = w_buf.at[m % 2]
        here = w[r]
        lap = w[r - 1] + w[r + 1] + pltpu.roll(here, 1, 0) + pltpu.roll(here, LON - 1, 0) - 4.0 * here
        u_buf[r] = jnp.where(H - 1 - m < step_count, c_buf[m % 2, r] + lap, u_buf[r])

    def two(row, m, first, second, count):
        def pair(i, carry):
            row(m, first + i)
            row(m, second + i)
            return carry

        if count > 0:
            lax.fori_loop(0, count, pair, 0)

    for m in range(H):
        inside = (R - 2 * m) // 2
        two(couple_row, m, H + m, H + m + inside, inside)
        inside = (R - 2 * m - 2) // 2
        two(spread_row, m, H + m + 1, H + m + 1 + inside, inside)
    got(seed_up, has_down)
    got(seed_down, has_up)

    def widen_seed(i, carry):
        u_buf[i] = seed_halo[0, i].astype(F32)
        u_buf[i + H + R] = seed_halo[1, i].astype(F32)
        return carry

    lax.fori_loop(0, H, widen_seed, 0)
    for m in range(H):
        two(couple_row, m, m, H + R - m, H)
        two(spread_row, m, m + 1, H + R - m - 1, H)

    got(end_on, has_prev)
    loads["prec"].wait()
    lane = lax.broadcasted_iota(jnp.int32, (MEM, MEM * LEV), 1)
    member = lax.broadcasted_iota(jnp.int32, (MEM, MEM * LEV), 0) * LEV
    own = jnp.where((lane >= member) & (lane < member + LEV), 1.0, 0.0).astype(BF16)

    for i in range(R):
        jump = prec[i].astype(F32) * (start[i] - end_prev[i].astype(F32))
        total = jump + u_buf[i + H]
        grad[i] = total
        terms = jnp.concatenate([(pert[k, i].astype(F32) * total).astype(BF16) for k in range(MEM)], axis=1)
        contrib[:, i * LANES:i * LANES + LON] = lax.dot_general(own, terms, LAST, preferred_element_type=F32)

    store = local(10, grad, grad_h.at[0])
    store.start()
    sums = lax.dot_general(halves(contrib[...]), onehot[...], LAST, preferred_element_type=F32)
    sums = sums[0:MEM] + sums[MEM:2 * MEM]
    for p in range(tm_count):
        term_send[p] = sums[:, p * CW:(p + 1) * CW]
    for d in range(1, tm_count):
        term(d).start()
    result = gathered[me_t] + term_send[me_t]
    for d in range(1, tm_count):
        term(d).wait_recv()
    for d in range(1, tm_count):
        result = result + term_recv[lax.rem(me_t + d, tm_count)]
    gw_ref[...] = result

    for d in range(1, tm_count):
        spread(d).wait_send()
        term(d).wait_send()
    for copy in (diff_up, state_up, seed_up):
        sent(copy, has_up)
    for copy in (diff_down, state_down, seed_down):
        sent(copy, has_down)
    sent(prec_back, has_prev)
    sent(start_back, has_prev)
    sent(end_on, has_next)
    store.wait()


def solution(mesh):
    tm_count, lat_count = mesh.shape["tm"], mesh.shape["lat"]

    def body(incr, pert, weight, cmap, steps, diffusion, m_in, m_out, prec, obs, innov):
        _, R, LON, LEV = incr.shape
        MEM, _, CW = weight.shape
        H = m_in.shape[0]
        PAD = -(-LON // 128) * 128
        field = lambda rows, kind: pltpu.VMEM((rows, LON, LEV), kind)
        wide = 2 * H + R
        scratch = [
            field(R, F32),
            pltpu.VMEM((MEM, R, LON, LEV), BF16),
            pltpu.VMEM((tm_count, MEM, CW), F32),
            pltpu.VMEM((R, LON), jnp.int32),
            pltpu.VMEM((R, PAD), jnp.int32),
            field(wide, BF16),
            pltpu.VMEM(m_in.shape, BF16),
            pltpu.VMEM(m_out.shape, BF16),
            field(R, BF16), field(R, BF16), field(R, BF16),
            pltpu.VMEM((CW * tm_count, R * PAD), BF16),
            field(R, F32), field(R, BF16), field(wide, F32), field(wide, F32),
            pltpu.VMEM((2, H, LON, LEV), BF16),
            field(R, BF16), field(R, BF16), field(R, BF16), field(R, BF16),
            field(wide, F32), field(R, BF16),
            pltpu.VMEM((2, H, LON, LEV), BF16),
            pltpu.VMEM((2, wide, LON, LEV), F32),
            pltpu.VMEM((2, wide, LON, LEV), F32),
            pltpu.VMEM((R * PAD, MEM), F32),
            pltpu.VMEM((MEM, R * PAD), F32),
            field(R, F32),
            pltpu.VMEM((tm_count, MEM, CW), F32),
            pltpu.VMEM((tm_count, MEM, CW), F32),
            pltpu.SemaphoreType.DMA((11,)),
            pltpu.SemaphoreType.DMA((9,)),
            pltpu.SemaphoreType.DMA((9,)),
        ] + [pltpu.SemaphoreType.DMA((tm_count,))] * 4

        def run(*refs):
            kernel(tm_count, lat_count, (H, R, LON, LEV, MEM, CW), *refs)

        grad, owned = pl.pallas_call(
            run,
            out_shape=(
                jax.ShapeDtypeStruct(incr.shape, F32),
                jax.ShapeDtypeStruct((MEM, CW), F32),
            ),
            in_specs=[pl.BlockSpec(memory_space=pltpu.SMEM)] + [pl.BlockSpec(memory_space=pl.ANY)] * 10,
            out_specs=(pl.BlockSpec(memory_space=pl.ANY), pl.BlockSpec(memory_space=pltpu.VMEM)),
            scratch_shapes=scratch,
            compiler_params=pltpu.CompilerParams(
                collective_id=0, has_side_effects=True, vmem_limit_bytes=60 * 1024 * 1024
            ),
        )(steps, incr, pert, weight[:, 0], cmap, diffusion, m_in, m_out, prec, obs, innov)
        return grad, owned[:, None]

    return jax.shard_map(
        body,
        mesh=mesh,
        in_specs=(
            P("tm", "lat", None, None),
            P(None, "tm", "lat", None, None),
            P(None, "lat", "tm"),
            P("lat", None),
            P("tm"),
            P("tm", "lat", None, None),
            P(),
            P(),
            P("tm", "lat", None, None),
            P("tm", "lat", None, None),
            P("tm", "lat", None, None),
        ),
        out_specs=(P("tm", "lat", None, None), P(None, "lat", "tm")),
        check_vma=False,
    )
```

```python
import jax
import jax.numpy as jnp
from jax import lax
from jax.experimental import pallas as pl
from jax.experimental.pallas import tpu as pltpu
from jax.sharding import PartitionSpec as P

MESH = pl.DeviceIdType.MESH
F32, BF16 = jnp.float32, jnp.bfloat16
GROUP = 2
LAST = (((1,), (1,)), ((), ()))


def halves(x):
    high = x.astype(BF16)
    low = (x - high.astype(F32)).astype(BF16)
    return jnp.concatenate([high, low], axis=0)


def kernel(
    tm_count, lat_count, sizes,
    steps_ref, incr_h, pert_h, weight_h, cmap_h, diff_h, min_h, mout_h, prec_h, obs_h, innov_h,
    grad_h, gw_ref,
    incr, pert, gathered, cmap, cpad, diff, m_in, m_out, prec, obs, innov,
    onehot, start, start_bf, a_buf, b_buf, state_halo, start_next, prec_next,
    end_bf, end_prev, u_buf, seed_bf, seed_halo, c_buf, w_buf, mw_t, contrib, grad,
    term_send, term_recv, local_sem, send_sem, recv_sem, ag_send, ag_recv, rs_send, rs_recv,
):
    H, R, LON, LEV, MEM, CW = sizes
    C = CW * tm_count
    PAD = cpad.shape[1]
    me_t, me_l = lax.axis_index("tm"), lax.axis_index("lat")
    has_up, has_down = me_l > 0, me_l < lat_count - 1
    has_prev, has_next = me_t > 0, me_t < tm_count - 1

    def local(i, src, dst):
        return pltpu.make_async_copy(src, dst, local_sem.at[i])

    def remote(i, src, dst, tm, lat):
        return pltpu.make_async_remote_copy(
            src_ref=src, dst_ref=dst, send_sem=send_sem.at[i], recv_sem=recv_sem.at[i],
            device_id=(tm, lat), device_id_type=MESH,
        )

    loads = dict(
        weight=local(0, weight_h, gathered.at[me_t]),
        cmap=local(1, cmap_h, cmap),
        pert=local(2, pert_h.at[:, 0], pert),
        incr=local(3, incr_h.at[0], incr),
        diff=local(4, diff_h.at[0], diff.at[pl.ds(H, R)]),
        m_in=local(5, min_h, m_in),
        m_out=local(6, mout_h, m_out),
        prec=local(7, prec_h.at[0], prec),
        obs=local(8, obs_h.at[0], obs),
        innov=local(9, innov_h.at[0], innov),
    )
    for copy in loads.values():
        copy.start()

    barrier = pltpu.get_barrier_semaphore()
    for d in range(1, tm_count):
        pl.semaphore_signal(barrier, inc=1, device_id=(lax.rem(me_t + d, tm_count), me_l), device_id_type=MESH)

    @pl.when(has_up)
    def _():
        pl.semaphore_signal(barrier, inc=1, device_id=(me_t, me_l - 1), device_id_type=MESH)

    @pl.when(has_down)
    def _():
        pl.semaphore_signal(barrier, inc=1, device_id=(me_t, me_l + 1), device_id_type=MESH)

    @pl.when(jnp.logical_not(has_up))
    def _():
        diff[0:H] = jnp.zeros((H, LON, LEV), BF16)
        state_halo[0] = jnp.zeros((H, LON, LEV), BF16)
        seed_halo[0] = jnp.zeros((H, LON, LEV), BF16)

    @pl.when(jnp.logical_not(has_down))
    def _():
        diff[H + R:2 * H + R] = jnp.zeros((H, LON, LEV), BF16)
        state_halo[1] = jnp.zeros((H, LON, LEV), BF16)
        seed_halo[1] = jnp.zeros((H, LON, LEV), BF16)

    @pl.when(jnp.logical_not(has_prev))
    def _():
        end_prev[...] = jnp.zeros((R, LON, LEV), BF16)

    @pl.when(jnp.logical_not(has_next))
    def _():
        start_next[...] = jnp.zeros((R, LON, LEV), BF16)
        prec_next[...] = jnp.zeros((R, LON, LEV), BF16)

    loads["weight"].wait()
    pl.semaphore_wait(barrier, tm_count - 1 + has_up.astype(jnp.int32) + has_down.astype(jnp.int32))

    def spread(d):
        peer = lax.rem(me_t + d, tm_count)
        return pltpu.make_async_remote_copy(
            src_ref=gathered.at[me_t], dst_ref=gathered.at[me_t], send_sem=ag_send.at[d],
            recv_sem=ag_recv.at[d], device_id=(peer, me_l), device_id_type=MESH,
        )

    def term(d):
        peer = lax.rem(me_t + d, tm_count)
        return pltpu.make_async_remote_copy(
            src_ref=term_send.at[peer], dst_ref=term_recv.at[me_t], send_sem=rs_send.at[d],
            recv_sem=rs_recv.at[d], device_id=(peer, me_l), device_id_type=MESH,
        )

    for d in range(1, tm_count):
        spread(d).start()

    diff_up = remote(0, diff_h.at[0, pl.ds(0, H)], diff.at[pl.ds(H + R, H)], me_t, me_l - 1)
    diff_down = remote(1, diff_h.at[0, pl.ds(R - H, H)], diff.at[pl.ds(0, H)], me_t, me_l + 1)
    prec_back = remote(2, prec_h.at[0], prec_next, me_t - 1, me_l)
    start_back = remote(3, start_bf, start_next, me_t - 1, me_l)
    state_up = remote(4, start_bf.at[pl.ds(0, H)], state_halo.at[1], me_t, me_l - 1)
    state_down = remote(5, start_bf.at[pl.ds(R - H, H)], state_halo.at[0], me_t, me_l + 1)
    end_on = remote(6, end_bf, end_prev, me_t + 1, me_l)
    seed_up = remote(7, seed_bf.at[pl.ds(0, H)], seed_halo.at[1], me_t, me_l - 1)
    seed_down = remote(8, seed_bf.at[pl.ds(R - H, H)], seed_halo.at[0], me_t, me_l + 1)

    def go(copy, there):
        @pl.when(there)
        def _():
            copy.start()

    def sent(copy, there):
        @pl.when(there)
        def _():
            copy.wait_send()

    def got(copy, there):
        @pl.when(there)
        def _():
            copy.wait_recv()

    go(diff_up, has_up)
    go(diff_down, has_down)
    go(prec_back, has_prev)

    loads["cmap"].wait()
    cpad[...] = jnp.full(cpad.shape, -1, jnp.int32)
    cpad[:, 0:LON] = cmap[...]
    contrib[...] = jnp.zeros(contrib.shape, F32)
    LANES = PAD
    CH = 128 if C % 128 == 0 else C

    def indicate(chunk, carry):
        base = pl.multiple_of(chunk * CH, CH)
        rows = lax.broadcasted_iota(jnp.int32, (CH, LANES), 0) + base
        for i in range(R):
            hit = jnp.where(rows == cpad[i:i + 1, :], 1.0, 0.0).astype(BF16)
            onehot[pl.ds(base, CH), i * LANES:(i + 1) * LANES] = hit
        return carry

    lax.fori_loop(0, C // CH, indicate, 0)

    for d in range(1, tm_count):
        spread(d).wait_recv()
    weights = jnp.concatenate([gathered[p] for p in range(tm_count)], axis=1)
    picked = jnp.dot(halves(weights), onehot[...], preferred_element_type=F32)
    mw_t[...] = jnp.transpose(picked[0:MEM] + picked[MEM:2 * MEM])

    loads["pert"].wait()
    loads["incr"].wait()

    def begin(i, carry):
        cols = mw_t[pl.ds(pl.multiple_of(i * LANES, LANES), LON), :]
        row = incr[i]
        for k in range(MEM):
            row = row + pert[k, i].astype(F32) * cols[:, k:k + 1]
        start[i] = row
        a_buf[i + H] = row
        start_bf[i] = row.astype(BF16)
        return carry

    lax.fori_loop(0, H, begin, 0)
    go(state_up, has_up)
    lax.fori_loop(H, R - H, begin, 0)
    lax.fori_loop(R - H, R, begin, 0)
    go(state_down, has_down)
    go(start_back, has_prev)

    step_count = steps_ref[0]
    loads["diff"].wait()
    loads["m_in"].wait()
    loads["m_out"].wait()

    def laplacian(field, r, count):
        here = field[pl.ds(r, count)]
        sides = pltpu.roll(here, 1, 1) + pltpu.roll(here, LON - 1, 1)
        return here, field[pl.ds(r - 1, count)] + field[pl.ds(r + 1, count)] + sides - 4.0 * here

    def forward_rows(n, src, dst, r, count):
        here, lap = laplacian(src, r, count)
        smoothed = here + diff[pl.ds(r, count)].astype(F32) * lap
        flat = smoothed.astype(BF16).reshape(count * LON, LEV)
        modes = jnp.dot(flat, m_in[n], preferred_element_type=F32).astype(BF16)
        moved = jnp.dot(modes, m_out[n], preferred_element_type=F32)
        advanced = smoothed + moved.reshape(count, LON, LEV)
        result = jnp.where(n < step_count, advanced, here)
        dst[pl.ds(r, count)] = result
        return result

    def buffers(n):
        return (a_buf, b_buf) if n % 2 == 0 else (b_buf, a_buf)

    def blocks(row, first, count):
        done = 0
        while done < count:
            size = min(GROUP, count - done)
            row(first + done, size)
            done += size

    def forward_inner(n):
        src, dst = buffers(n)
        blocks(lambda r, c: forward_rows(n, src, dst, r, c), H + n + 1, R - 2 * n - 2)

    def forward_edges(n):
        src, dst = buffers(n)
        blocks(lambda r, c: forward_rows(n, src, dst, r, c), n + 1, H)
        blocks(lambda r, c: forward_rows(n, src, dst, r, c), H + R - n - 1, H)

    for n in range(H - 1):
        forward_inner(n)
    got(diff_up, has_down)
    got(diff_down, has_up)
    got(state_up, has_down)
    got(state_down, has_up)

    def widen(i, carry):
        a_buf[i] = state_halo[0, i].astype(F32)
        a_buf[i + H + R] = state_halo[1, i].astype(F32)
        return carry

    lax.fori_loop(0, H, widen, 0)
    for n in range(H - 1):
        forward_edges(n)
    loads["obs"].wait()
    loads["innov"].wait()
    got(prec_back, has_next)
    got(start_back, has_next)
    src, dst = buffers(H - 1)

    def finish(i, count):
        rows = pl.ds(i, count)
        end = forward_rows(H - 1, src, dst, i + H, count)
        misfit = obs[rows].astype(F32) * (end - innov[rows].astype(F32))
        seed = misfit - prec_next[rows].astype(F32) * (start_next[rows].astype(F32) - end)
        end_bf[rows] = end.astype(BF16)
        u_buf[pl.ds(i + H, count)] = seed
        seed_bf[rows] = seed.astype(BF16)

    blocks(finish, 0, H)
    go(seed_up, has_up)
    blocks(finish, H, R - H)
    go(seed_down, has_down)
    go(end_on, has_next)

    def couple(m, r, count):
        n = H - 1 - m
        rows = pl.ds(r, count)
        here = u_buf[rows]
        flat = here.astype(BF16).reshape(count * LON, LEV)
        modes = lax.dot_general(flat, m_out[n], LAST, preferred_element_type=F32).astype(BF16)
        moved = lax.dot_general(modes, m_in[n], LAST, preferred_element_type=F32)
        coupled = here + moved.reshape(count, LON, LEV)
        c_buf[m % 2, rows] = coupled
        w_buf[m % 2, rows] = diff[rows].astype(F32) * coupled

    def settle(m, r, count):
        rows = pl.ds(r, count)
        _, lap = laplacian(w_buf.at[m % 2], r, count)
        u_buf[rows] = jnp.where(H - 1 - m < step_count, c_buf[m % 2, rows] + lap, u_buf[rows])

    for m in range(H):
        blocks(lambda r, c: couple(m, r, c), H + m, R - 2 * m)
        blocks(lambda r, c: settle(m, r, c), H + m + 1, R - 2 * m - 2)
    got(seed_up, has_down)
    got(seed_down, has_up)

    def widen_seed(i, carry):
        u_buf[i] = seed_halo[0, i].astype(F32)
        u_buf[i + H + R] = seed_halo[1, i].astype(F32)
        return carry

    lax.fori_loop(0, H, widen_seed, 0)
    for m in range(H):
        blocks(lambda r, c: couple(m, r, c), m, H)
        blocks(lambda r, c: couple(m, r, c), H + R - m, H)
        blocks(lambda r, c: settle(m, r, c), m + 1, H)
        blocks(lambda r, c: settle(m, r, c), H + R - m - 1, H)

    got(end_on, has_prev)
    loads["prec"].wait()
    lane = lax.broadcasted_iota(jnp.int32, (MEM, MEM * LEV), 1)
    member = lax.broadcasted_iota(jnp.int32, (MEM, MEM * LEV), 0) * LEV
    own = jnp.where((lane >= member) & (lane < member + LEV), 1.0, 0.0).astype(BF16)

    for i in range(R):
        jump = prec[i].astype(F32) * (start[i] - end_prev[i].astype(F32))
        total = jump + u_buf[i + H]
        grad[i] = total
        terms = jnp.concatenate([(pert[k, i].astype(F32) * total).astype(BF16) for k in range(MEM)], axis=1)
        contrib[:, i * LANES:i * LANES + LON] = lax.dot_general(own, terms, LAST, preferred_element_type=F32)

    store = local(10, grad, grad_h.at[0])
    store.start()
    sums = lax.dot_general(halves(contrib[...]), onehot[...], LAST, preferred_element_type=F32)
    sums = sums[0:MEM] + sums[MEM:2 * MEM]
    for p in range(tm_count):
        term_send[p] = sums[:, p * CW:(p + 1) * CW]
    for d in range(1, tm_count):
        term(d).start()
    result = gathered[me_t] + term_send[me_t]
    for d in range(1, tm_count):
        term(d).wait_recv()
    for d in range(1, tm_count):
        result = result + term_recv[lax.rem(me_t + d, tm_count)]
    gw_ref[...] = result

    for d in range(1, tm_count):
        spread(d).wait_send()
        term(d).wait_send()
    for copy in (diff_up, state_up, seed_up):
        sent(copy, has_up)
    for copy in (diff_down, state_down, seed_down):
        sent(copy, has_down)
    sent(prec_back, has_prev)
    sent(start_back, has_prev)
    sent(end_on, has_next)
    store.wait()


def deliver(grad_h, owned_h, out_h, gw_ref, buf, small, sem_in, sem_out, sem_small):
    R = buf.shape[0]
    pieces = 4 if R % 4 == 0 else 1
    size = R // pieces
    ins, outs = [], []
    for i in range(pieces):
        rows = pl.ds(i * size, size)
        ins.append(pltpu.make_async_copy(grad_h.at[0, rows], buf.at[rows], sem_in.at[i]))
        outs.append(pltpu.make_async_copy(buf.at[rows], out_h.at[0, rows], sem_out.at[i]))
    fetch = pltpu.make_async_copy(owned_h, small, sem_small.at[0])
    for copy in ins:
        copy.start()
    fetch.start()
    for arrive, leave in zip(ins, outs):
        arrive.wait()
        leave.start()
    fetch.wait()
    gw_ref[:, 0, :] = small[...]
    for copy in outs:
        copy.wait()


def solution(mesh):
    tm_count, lat_count = mesh.shape["tm"], mesh.shape["lat"]

    def body(incr, pert, weight, cmap, steps, diffusion, m_in, m_out, prec, obs, innov):
        _, R, LON, LEV = incr.shape
        MEM, _, CW = weight.shape
        H = m_in.shape[0]
        PAD = -(-LON // 128) * 128
        field = lambda rows, kind: pltpu.VMEM((rows, LON, LEV), kind)
        wide = 2 * H + R
        scratch = [
            field(R, F32),
            pltpu.VMEM((MEM, R, LON, LEV), BF16),
            pltpu.VMEM((tm_count, MEM, CW), F32),
            pltpu.VMEM((R, LON), jnp.int32),
            pltpu.VMEM((R, PAD), jnp.int32),
            field(wide, BF16),
            pltpu.VMEM(m_in.shape, BF16),
            pltpu.VMEM(m_out.shape, BF16),
            field(R, BF16), field(R, BF16), field(R, BF16),
            pltpu.VMEM((CW * tm_count, R * PAD), BF16),
            field(R, F32), field(R, BF16), field(wide, F32), field(wide, F32),
            pltpu.VMEM((2, H, LON, LEV), BF16),
            field(R, BF16), field(R, BF16), field(R, BF16), field(R, BF16),
            field(wide, F32), field(R, BF16),
            pltpu.VMEM((2, H, LON, LEV), BF16),
            pltpu.VMEM((2, wide, LON, LEV), F32),
            pltpu.VMEM((2, wide, LON, LEV), F32),
            pltpu.VMEM((R * PAD, MEM), F32),
            pltpu.VMEM((MEM, R * PAD), F32),
            field(R, F32),
            pltpu.VMEM((tm_count, MEM, CW), F32),
            pltpu.VMEM((tm_count, MEM, CW), F32),
            pltpu.SemaphoreType.DMA((11,)),
            pltpu.SemaphoreType.DMA((9,)),
            pltpu.SemaphoreType.DMA((9,)),
        ] + [pltpu.SemaphoreType.DMA((tm_count,))] * 4

        def run(*refs):
            kernel(tm_count, lat_count, (H, R, LON, LEV, MEM, CW), *refs)

        grad, owned = pl.pallas_call(
            run,
            out_shape=(
                jax.ShapeDtypeStruct(incr.shape, F32),
                jax.ShapeDtypeStruct((MEM, CW), F32),
            ),
            in_specs=[pl.BlockSpec(memory_space=pltpu.SMEM)] + [pl.BlockSpec(memory_space=pl.ANY)] * 10,
            out_specs=(pl.BlockSpec(memory_space=pl.ANY), pl.BlockSpec(memory_space=pltpu.VMEM)),
            scratch_shapes=scratch,
            compiler_params=pltpu.CompilerParams(
                collective_id=0, has_side_effects=True, vmem_limit_bytes=60 * 1024 * 1024
            ),
        )(steps, incr, pert, weight[:, 0], cmap, diffusion, m_in, m_out, prec, obs, innov)
        return pl.pallas_call(
            deliver,
            out_shape=(
                jax.ShapeDtypeStruct(incr.shape, F32),
                jax.ShapeDtypeStruct((MEM, 1, CW), F32),
            ),
            in_specs=[pl.BlockSpec(memory_space=pl.ANY)] * 2,
            out_specs=(pl.BlockSpec(memory_space=pl.ANY), pl.BlockSpec(memory_space=pltpu.VMEM)),
            scratch_shapes=[
                field(R, F32),
                pltpu.VMEM((MEM, CW), F32),
                pltpu.SemaphoreType.DMA((4,)),
                pltpu.SemaphoreType.DMA((4,)),
                pltpu.SemaphoreType.DMA((1,)),
            ],
        )(grad, owned)

    return jax.shard_map(
        body,
        mesh=mesh,
        in_specs=(
            P("tm", "lat", None, None),
            P(None, "tm", "lat", None, None),
            P(None, "lat", "tm"),
            P("lat", None),
            P("tm"),
            P("tm", "lat", None, None),
            P(),
            P(),
            P("tm", "lat", None, None),
            P("tm", "lat", None, None),
            P("tm", "lat", None, None),
        ),
        out_specs=(P("tm", "lat", None, None), P(None, "lat", "tm")),
        check_vma=False,
    )
```

```python
import jax
import jax.numpy as jnp
from jax import lax
from jax.experimental import pallas as pl
from jax.experimental.pallas import tpu as pltpu
from jax.sharding import PartitionSpec as P

MESH = pl.DeviceIdType.MESH
F32, BF16 = jnp.float32, jnp.bfloat16
GROUP = 2
LAST = (((1,), (1,)), ((), ()))


def halves(x):
    high = x.astype(BF16)
    low = (x - high.astype(F32)).astype(BF16)
    return jnp.concatenate([high, low], axis=0)


def kernel(
    tm_count, lat_count, sizes,
    steps_ref, incr_h, pert_h, weight_h, cmap_h, diff_h, min_h, mout_h, prec_h, obs_h, innov_h,
    grad_h, gw_ref,
    incr, pert, gathered, cmap, cpad, diff, m_in, m_out, prec, obs, innov,
    onehot, start, start_bf, a_buf, b_buf, state_halo, start_next, prec_next,
    end_bf, end_prev, u_buf, seed_bf, seed_halo, c_buf, w_buf, mw_t, contrib, grad,
    term_send, term_recv, local_sem, send_sem, recv_sem, ag_send, ag_recv, rs_send, rs_recv,
):
    H, R, LON, LEV, MEM, CW = sizes
    C = CW * tm_count
    PAD = cpad.shape[1]
    me_t, me_l = lax.axis_index("tm"), lax.axis_index("lat")
    has_up, has_down = me_l > 0, me_l < lat_count - 1
    has_prev, has_next = me_t > 0, me_t < tm_count - 1

    def local(i, src, dst):
        return pltpu.make_async_copy(src, dst, local_sem.at[i])

    def remote(i, src, dst, tm, lat):
        return pltpu.make_async_remote_copy(
            src_ref=src, dst_ref=dst, send_sem=send_sem.at[i], recv_sem=recv_sem.at[i],
            device_id=(tm, lat), device_id_type=MESH,
        )

    loads = dict(
        weight=local(0, weight_h, gathered.at[me_t]),
        cmap=local(1, cmap_h, cmap),
        pert=local(2, pert_h.at[:, 0], pert),
        incr=local(3, incr_h.at[0], incr),
        diff=local(4, diff_h.at[0], diff.at[pl.ds(H, R)]),
        m_in=local(5, min_h, m_in),
        m_out=local(6, mout_h, m_out),
        prec=local(7, prec_h.at[0], prec),
        obs=local(8, obs_h.at[0], obs),
        innov=local(9, innov_h.at[0], innov),
    )
    for copy in loads.values():
        copy.start()

    barrier = pltpu.get_barrier_semaphore()
    for d in range(1, tm_count):
        pl.semaphore_signal(barrier, inc=1, device_id=(lax.rem(me_t + d, tm_count), me_l), device_id_type=MESH)

    @pl.when(has_up)
    def _():
        pl.semaphore_signal(barrier, inc=1, device_id=(me_t, me_l - 1), device_id_type=MESH)

    @pl.when(has_down)
    def _():
        pl.semaphore_signal(barrier, inc=1, device_id=(me_t, me_l + 1), device_id_type=MESH)

    @pl.when(jnp.logical_not(has_up))
    def _():
        diff[0:H] = jnp.zeros((H, LON, LEV), BF16)
        state_halo[0] = jnp.zeros((H, LON, LEV), BF16)
        seed_halo[0] = jnp.zeros((H, LON, LEV), BF16)

    @pl.when(jnp.logical_not(has_down))
    def _():
        diff[H + R:2 * H + R] = jnp.zeros((H, LON, LEV), BF16)
        state_halo[1] = jnp.zeros((H, LON, LEV), BF16)
        seed_halo[1] = jnp.zeros((H, LON, LEV), BF16)

    @pl.when(jnp.logical_not(has_prev))
    def _():
        end_prev[...] = jnp.zeros((R, LON, LEV), BF16)

    @pl.when(jnp.logical_not(has_next))
    def _():
        start_next[...] = jnp.zeros((R, LON, LEV), BF16)
        prec_next[...] = jnp.zeros((R, LON, LEV), BF16)

    loads["weight"].wait()
    pl.semaphore_wait(barrier, tm_count - 1 + has_up.astype(jnp.int32) + has_down.astype(jnp.int32))

    def spread(d):
        peer = lax.rem(me_t + d, tm_count)
        return pltpu.make_async_remote_copy(
            src_ref=gathered.at[me_t], dst_ref=gathered.at[me_t], send_sem=ag_send.at[d],
            recv_sem=ag_recv.at[d], device_id=(peer, me_l), device_id_type=MESH,
        )

    def term(d):
        peer = lax.rem(me_t + d, tm_count)
        return pltpu.make_async_remote_copy(
            src_ref=term_send.at[peer], dst_ref=term_recv.at[me_t], send_sem=rs_send.at[d],
            recv_sem=rs_recv.at[d], device_id=(peer, me_l), device_id_type=MESH,
        )

    for d in range(1, tm_count):
        spread(d).start()

    diff_up = remote(0, diff_h.at[0, pl.ds(0, H)], diff.at[pl.ds(H + R, H)], me_t, me_l - 1)
    diff_down = remote(1, diff_h.at[0, pl.ds(R - H, H)], diff.at[pl.ds(0, H)], me_t, me_l + 1)
    prec_back = remote(2, prec_h.at[0], prec_next, me_t - 1, me_l)
    start_back = remote(3, start_bf, start_next, me_t - 1, me_l)
    end_on = remote(4, end_bf, end_prev, me_t + 1, me_l)
    Q = GROUP if H % GROUP == 0 else 1
    parts = H // Q

    def edge_copies(base, field, halo):
        ups, downs = [], []
        for c in range(parts):
            first = c * Q
            ups.append(remote(base + c, field.at[pl.ds(first, Q)], halo.at[1, pl.ds(first, Q)], me_t, me_l - 1))
            first = H - (c + 1) * Q
            downs.append(remote(
                base + parts + c, field.at[pl.ds(R - H + first, Q)], halo.at[0, pl.ds(first, Q)], me_t, me_l + 1
            ))
        return ups, downs

    state_up, state_down = edge_copies(5, start_bf, state_halo)
    seed_up, seed_down = edge_copies(5 + 2 * parts, seed_bf, seed_halo)

    def go(copy, there):
        @pl.when(there)
        def _():
            copy.start()

    def sent(copy, there):
        @pl.when(there)
        def _():
            copy.wait_send()

    def got(copy, there):
        @pl.when(there)
        def _():
            copy.wait_recv()

    go(diff_up, has_up)
    go(diff_down, has_down)
    go(prec_back, has_prev)

    loads["cmap"].wait()
    cpad[...] = jnp.full(cpad.shape, -1, jnp.int32)
    cpad[:, 0:LON] = cmap[...]
    contrib[...] = jnp.zeros(contrib.shape, F32)
    LANES = PAD
    CH = 128 if C % 128 == 0 else C

    def indicate(chunk, carry):
        base = pl.multiple_of(chunk * CH, CH)
        rows = lax.broadcasted_iota(jnp.int32, (CH, LANES), 0) + base
        for i in range(R):
            hit = jnp.where(rows == cpad[i:i + 1, :], 1.0, 0.0).astype(BF16)
            onehot[pl.ds(base, CH), i * LANES:(i + 1) * LANES] = hit
        return carry

    lax.fori_loop(0, C // CH, indicate, 0)

    for d in range(1, tm_count):
        spread(d).wait_recv()
    weights = jnp.concatenate([gathered[p] for p in range(tm_count)], axis=1)
    picked = jnp.dot(halves(weights), onehot[...], preferred_element_type=F32)
    mw_t[...] = jnp.transpose(picked[0:MEM] + picked[MEM:2 * MEM])

    loads["pert"].wait()
    loads["incr"].wait()

    def begin(first, count):
        for i in range(first, first + count):
            cols = mw_t[i * LANES:i * LANES + LON, :]
            row = incr[i]
            for k in range(MEM):
                row = row + pert[k, i].astype(F32) * cols[:, k:k + 1]
            start[i] = row
            a_buf[i + H] = row
            start_bf[i] = row.astype(BF16)

    def blocks(row, first, count):
        done = 0
        while done < count:
            size = min(GROUP, count - done)
            row(first + done, size)
            done += size

    def from_edges(row, ups, downs):
        for c in range(parts):
            row(c * Q, Q)
            go(ups[c], has_up)
            row(R - (c + 1) * Q, Q)
            go(downs[c], has_down)
        blocks(row, H, R - 2 * H)

    from_edges(begin, state_up, state_down)
    go(start_back, has_prev)

    step_count = steps_ref[0]
    loads["diff"].wait()
    loads["m_in"].wait()
    loads["m_out"].wait()

    def laplacian(field, r, count):
        here = field[pl.ds(r, count)]
        sides = pltpu.roll(here, 1, 1) + pltpu.roll(here, LON - 1, 1)
        return here, field[pl.ds(r - 1, count)] + field[pl.ds(r + 1, count)] + sides - 4.0 * here

    def forward_rows(n, src, dst, r, count):
        here, lap = laplacian(src, r, count)
        smoothed = here + diff[pl.ds(r, count)].astype(F32) * lap
        flat = smoothed.astype(BF16).reshape(count * LON, LEV)
        modes = jnp.dot(flat, m_in[n], preferred_element_type=F32).astype(BF16)
        moved = jnp.dot(modes, m_out[n], preferred_element_type=F32)
        advanced = smoothed + moved.reshape(count, LON, LEV)
        result = jnp.where(n < step_count, advanced, here)
        dst[pl.ds(r, count)] = result
        return result

    def buffers(n):
        return (a_buf, b_buf) if n % 2 == 0 else (b_buf, a_buf)

    def forward_inner(n):
        src, dst = buffers(n)
        blocks(lambda r, c: forward_rows(n, src, dst, r, c), H + n + 1, R - 2 * n - 2)

    def forward_edges(n):
        src, dst = buffers(n)
        blocks(lambda r, c: forward_rows(n, src, dst, r, c), n + 1, H)
        blocks(lambda r, c: forward_rows(n, src, dst, r, c), H + R - n - 1, H)

    for n in range(H - 1):
        forward_inner(n)
    got(diff_up, has_down)
    got(diff_down, has_up)
    for copy in state_up:
        got(copy, has_down)
    for copy in state_down:
        got(copy, has_up)

    def widen(i, carry):
        a_buf[i] = state_halo[0, i].astype(F32)
        a_buf[i + H + R] = state_halo[1, i].astype(F32)
        return carry

    lax.fori_loop(0, H, widen, 0)
    for n in range(H - 1):
        forward_edges(n)
    loads["obs"].wait()
    loads["innov"].wait()
    got(prec_back, has_next)
    got(start_back, has_next)
    src, dst = buffers(H - 1)

    def finish(i, count):
        rows = pl.ds(i, count)
        end = forward_rows(H - 1, src, dst, i + H, count)
        misfit = obs[rows].astype(F32) * (end - innov[rows].astype(F32))
        seed = misfit - prec_next[rows].astype(F32) * (start_next[rows].astype(F32) - end)
        end_bf[rows] = end.astype(BF16)
        u_buf[pl.ds(i + H, count)] = seed
        seed_bf[rows] = seed.astype(BF16)

    from_edges(finish, seed_up, seed_down)
    go(end_on, has_next)

    def couple(m, r, count):
        n = H - 1 - m
        rows = pl.ds(r, count)
        here = u_buf[rows]
        flat = here.astype(BF16).reshape(count * LON, LEV)
        modes = lax.dot_general(flat, m_out[n], LAST, preferred_element_type=F32).astype(BF16)
        moved = lax.dot_general(modes, m_in[n], LAST, preferred_element_type=F32)
        coupled = here + moved.reshape(count, LON, LEV)
        c_buf[m % 2, rows] = coupled
        w_buf[m % 2, rows] = diff[rows].astype(F32) * coupled

    def settle(m, r, count):
        rows = pl.ds(r, count)
        _, lap = laplacian(w_buf.at[m % 2], r, count)
        u_buf[rows] = jnp.where(H - 1 - m < step_count, c_buf[m % 2, rows] + lap, u_buf[rows])

    for m in range(H):
        blocks(lambda r, c: couple(m, r, c), H + m, R - 2 * m)
        blocks(lambda r, c: settle(m, r, c), H + m + 1, R - 2 * m - 2)
    for copy in seed_up:
        got(copy, has_down)
    for copy in seed_down:
        got(copy, has_up)

    def widen_seed(i, carry):
        u_buf[i] = seed_halo[0, i].astype(F32)
        u_buf[i + H + R] = seed_halo[1, i].astype(F32)
        return carry

    lax.fori_loop(0, H, widen_seed, 0)
    for m in range(H):
        blocks(lambda r, c: couple(m, r, c), m, H)
        blocks(lambda r, c: couple(m, r, c), H + R - m, H)
        blocks(lambda r, c: settle(m, r, c), m + 1, H)
        blocks(lambda r, c: settle(m, r, c), H + R - m - 1, H)

    got(end_on, has_prev)
    loads["prec"].wait()
    lane = lax.broadcasted_iota(jnp.int32, (MEM, MEM * LEV), 1)
    member = lax.broadcasted_iota(jnp.int32, (MEM, MEM * LEV), 0) * LEV
    own = jnp.where((lane >= member) & (lane < member + LEV), 1.0, 0.0).astype(BF16)

    for i in range(R):
        jump = prec[i].astype(F32) * (start[i] - end_prev[i].astype(F32))
        total = jump + u_buf[i + H]
        grad[i] = total
        terms = jnp.concatenate([(pert[k, i].astype(F32) * total).astype(BF16) for k in range(MEM)], axis=1)
        contrib[:, i * LANES:i * LANES + LON] = lax.dot_general(own, terms, LAST, preferred_element_type=F32)

    store = local(10, grad, grad_h.at[0])
    store.start()
    pieces = halves(contrib[...])

    def owed(p):
        block = onehot[pl.ds(pl.multiple_of(p * CW, CW), CW), :]
        both = lax.dot_general(pieces, block, LAST, preferred_element_type=F32)
        return both[0:MEM] + both[MEM:2 * MEM]

    for d in sorted(range(1, tm_count), key=lambda d: -min(d, tm_count - d)):
        peer = lax.rem(me_t + d, tm_count)
        term_send[peer] = owed(peer)
        term(d).start()
    result = gathered[me_t] + owed(me_t)
    for d in range(1, tm_count):
        term(d).wait_recv()
    for d in range(1, tm_count):
        result = result + term_recv[lax.rem(me_t + d, tm_count)]
    gw_ref[...] = result

    for d in range(1, tm_count):
        spread(d).wait_send()
        term(d).wait_send()
    for copy in [diff_up] + state_up + seed_up:
        sent(copy, has_up)
    for copy in [diff_down] + state_down + seed_down:
        sent(copy, has_down)
    sent(prec_back, has_prev)
    sent(start_back, has_prev)
    sent(end_on, has_next)
    store.wait()


def deliver(grad_h, owned_h, out_h, gw_ref, buf, small, sem_in, sem_out, sem_small):
    R = buf.shape[0]
    pieces = 4 if R % 4 == 0 else 1
    size = R // pieces
    ins, outs = [], []
    for i in range(pieces):
        rows = pl.ds(i * size, size)
        ins.append(pltpu.make_async_copy(grad_h.at[0, rows], buf.at[rows], sem_in.at[i]))
        outs.append(pltpu.make_async_copy(buf.at[rows], out_h.at[0, rows], sem_out.at[i]))
    fetch = pltpu.make_async_copy(owned_h, small, sem_small.at[0])
    for copy in ins:
        copy.start()
    fetch.start()
    for arrive, leave in zip(ins, outs):
        arrive.wait()
        leave.start()
    fetch.wait()
    gw_ref[:, 0, :] = small[...]
    for copy in outs:
        copy.wait()


def solution(mesh):
    tm_count, lat_count = mesh.shape["tm"], mesh.shape["lat"]

    def body(incr, pert, weight, cmap, steps, diffusion, m_in, m_out, prec, obs, innov):
        _, R, LON, LEV = incr.shape
        MEM, _, CW = weight.shape
        H = m_in.shape[0]
        PAD = -(-LON // 128) * 128
        field = lambda rows, kind: pltpu.VMEM((rows, LON, LEV), kind)
        wide = 2 * H + R
        scratch = [
            field(R, F32),
            pltpu.VMEM((MEM, R, LON, LEV), BF16),
            pltpu.VMEM((tm_count, MEM, CW), F32),
            pltpu.VMEM((R, LON), jnp.int32),
            pltpu.VMEM((R, PAD), jnp.int32),
            field(wide, BF16),
            pltpu.VMEM(m_in.shape, BF16),
            pltpu.VMEM(m_out.shape, BF16),
            field(R, BF16), field(R, BF16), field(R, BF16),
            pltpu.VMEM((CW * tm_count, R * PAD), BF16),
            field(R, F32), field(R, BF16), field(wide, F32), field(wide, F32),
            pltpu.VMEM((2, H, LON, LEV), BF16),
            field(R, BF16), field(R, BF16), field(R, BF16), field(R, BF16),
            field(wide, F32), field(R, BF16),
            pltpu.VMEM((2, H, LON, LEV), BF16),
            pltpu.VMEM((2, wide, LON, LEV), F32),
            pltpu.VMEM((2, wide, LON, LEV), F32),
            pltpu.VMEM((R * PAD, MEM), F32),
            pltpu.VMEM((MEM, R * PAD), F32),
            field(R, F32),
            pltpu.VMEM((tm_count, MEM, CW), F32),
            pltpu.VMEM((tm_count, MEM, CW), F32),
            pltpu.SemaphoreType.DMA((11,)),
            pltpu.SemaphoreType.DMA((5 + 4 * H,)),
            pltpu.SemaphoreType.DMA((5 + 4 * H,)),
        ] + [pltpu.SemaphoreType.DMA((tm_count,))] * 4

        def run(*refs):
            kernel(tm_count, lat_count, (H, R, LON, LEV, MEM, CW), *refs)

        grad, owned = pl.pallas_call(
            run,
            out_shape=(
                jax.ShapeDtypeStruct(incr.shape, F32),
                jax.ShapeDtypeStruct((MEM, CW), F32),
            ),
            in_specs=[pl.BlockSpec(memory_space=pltpu.SMEM)] + [pl.BlockSpec(memory_space=pl.ANY)] * 10,
            out_specs=(pl.BlockSpec(memory_space=pl.ANY), pl.BlockSpec(memory_space=pltpu.VMEM)),
            scratch_shapes=scratch,
            compiler_params=pltpu.CompilerParams(
                collective_id=0, has_side_effects=True, vmem_limit_bytes=60 * 1024 * 1024
            ),
        )(steps, incr, pert, weight[:, 0], cmap, diffusion, m_in, m_out, prec, obs, innov)
        return pl.pallas_call(
            deliver,
            out_shape=(
                jax.ShapeDtypeStruct(incr.shape, F32),
                jax.ShapeDtypeStruct((MEM, 1, CW), F32),
            ),
            in_specs=[pl.BlockSpec(memory_space=pl.ANY)] * 2,
            out_specs=(pl.BlockSpec(memory_space=pl.ANY), pl.BlockSpec(memory_space=pltpu.VMEM)),
            scratch_shapes=[
                field(R, F32),
                pltpu.VMEM((MEM, CW), F32),
                pltpu.SemaphoreType.DMA((4,)),
                pltpu.SemaphoreType.DMA((4,)),
                pltpu.SemaphoreType.DMA((1,)),
            ],
        )(grad, owned)

    return jax.shard_map(
        body,
        mesh=mesh,
        in_specs=(
            P("tm", "lat", None, None),
            P(None, "tm", "lat", None, None),
            P(None, "lat", "tm"),
            P("lat", None),
            P("tm"),
            P("tm", "lat", None, None),
            P(),
            P(),
            P("tm", "lat", None, None),
            P("tm", "lat", None, None),
            P("tm", "lat", None, None),
        ),
        out_specs=(P("tm", "lat", None, None), P(None, "lat", "tm")),
        check_vma=False,
    )
```
